32 devices in a mesh: space: 4 (over y, x), tm: 8 (over z, core).
Axes of the slice: x: 2, y: 2, z: 4, core: 2. Of those that a mesh axis runs over, the one named last changes fastest.
Arguments:
- snapshots: float32 [4096, 4096], P('space', 'tm'), may hold values from -6 to 6
- test_seeds: int32 [2], replicated, may hold values from 0 to 16777215
- block_offsets: int32 [2], replicated, may hold values from 0 to 4095
Outputs:
- residual: float32 [4096, 4096], P('space', 'tm')
- factor: float32 [512, 512], replicated
The draws below stay inside these ranges and needn't reach their ends.
Inputs may be any that keep to these rules, and one draw needn't show every extreme that they name: `test_seeds`: seeds of the two test matrices.
All inputs are finite; a program needn't handle non-finite values.
Results may differ from the reference program's by a relative error of at most 0.0003.
Values sent between devices are 32-bit elements; how exact they have to be, the bound alone decides.
A program may use at most 128 MiB of HBM per device.

```python
import math
import jax
import jax.numpy as jnp
from jax import lax

RANGE = 512
CORANGE = 1024
CELLS = 4096
SNAPS = 4096


def shard_levels(stream_key, dims, shards, least, largest):
    level = 1.0
    for position, blocks in shards:
        steps = jax.random.uniform(jax.random.fold_in(jax.random.fold_in(stream_key, 6), position), (blocks,), jnp.float32, least / len(shards), largest / len(shards))
        level = level * jnp.repeat(jnp.exp(steps), dims[position] // blocks).reshape((-1,) + (1,) * (len(dims) - 1 - position))
    return level


def gaussian(key, shape, scale, reach, split=(), kind=jnp.bfloat16):
    factor_of = shard_levels(key, shape, split, -0.22, 0.18) if split else 1.0
    entries = jax.random.normal(key, shape, jnp.float32) * scale * factor_of
    return jnp.minimum(jnp.maximum(entries, -reach), reach).astype(kind)


def setup_inputs(seed: int = 0) -> dict:
    seeds = jax.random.split(jax.random.key(seed), 4)
    return {
        "snapshots": gaussian(seeds[0], (CELLS, SNAPS), 1.0, 6.0, ((0, 4), (1, 8)), jnp.float32),
        "test_seeds": jax.random.randint(seeds[1], (2,), 0, 16777216).astype(jnp.int32),
        "block_offsets": jax.random.randint(seeds[2], (2,), 0, 4096).astype(jnp.int32),
    }


PRECISE = lax.Precision.HIGHEST

def scramble(values):
    values = jnp.bitwise_xor(values, lax.shift_right_logical(values, jnp.int32(16)))
    values = values * 73244475
    values = jnp.bitwise_xor(values, lax.shift_right_logical(values, jnp.int32(16)))
    values = values * 73244475
    values = jnp.bitwise_xor(values, lax.shift_right_logical(values, jnp.int32(16)))
    return values

def gaussian_table(row_ids, col_ids, seed_value):
    row_hash = scramble(row_ids * 668265261 + seed_value)
    cell_hash = scramble(jnp.bitwise_xor(row_hash[:, None], col_ids[None, :] * 374761393))
    running = jnp.zeros(cell_hash.shape, jnp.float32)
    for stream in range(4):
        hashed = scramble(cell_hash + stream * 625341585)
        running = running + jnp.bitwise_and(hashed, 16777215).astype(jnp.float32) * (1.0 / 16777216.0)
    return (running - 2.0) * math.sqrt(3.0)

def reference(snapshots, test_seeds, block_offsets):
    cell_ids = block_offsets[0] * CELLS + jnp.arange(CELLS, dtype=jnp.int32)
    snap_ids = block_offsets[1] * SNAPS + jnp.arange(SNAPS, dtype=jnp.int32)
    omega_test = gaussian_table(snap_ids, jnp.arange(RANGE, dtype=jnp.int32), test_seeds[0]) / math.sqrt(CELLS * SNAPS)
    psi_test = gaussian_table(cell_ids, jnp.arange(CORANGE, dtype=jnp.int32), test_seeds[1]) / math.sqrt(CELLS)
    range_sketch = jnp.dot(snapshots, omega_test, precision=PRECISE)
    corange_sketch = jnp.dot(psi_test.T, snapshots, precision=PRECISE)
    range_basis, factor = jnp.linalg.qr(range_sketch)
    sign_fix = jnp.where(jnp.diagonal(factor) < 0, -1.0, 1.0).astype(jnp.float32)
    range_basis = range_basis * sign_fix[None, :]
    factor = factor * sign_fix[:, None]
    coupling = jnp.dot(psi_test.T, range_basis, precision=PRECISE)
    normal = jnp.dot(coupling.T, coupling, precision=PRECISE)
    core_factor = jnp.linalg.cholesky(normal)
    projected = jnp.dot(coupling.T, corange_sketch, precision=PRECISE)
    core_matrix = jax.scipy.linalg.cho_solve((core_factor, True), projected)
    residual = snapshots - jnp.dot(range_basis, core_matrix, precision=PRECISE)
    return (residual, factor)
```

```python
import math

import jax
import jax.numpy as jnp
from jax import lax
from jax.experimental import pallas as pl
from jax.experimental.pallas import tpu as pltpu
from jax.sharding import PartitionSpec as P

RANGE = 512
CORANGE = 1024
BLOCK = 32

PRECISE = lax.Precision.HIGHEST


def scramble(values):
    values = jnp.bitwise_xor(values, lax.shift_right_logical(values, jnp.int32(16)))
    values = values * 73244475
    values = jnp.bitwise_xor(values, lax.shift_right_logical(values, jnp.int32(16)))
    values = values * 73244475
    values = jnp.bitwise_xor(values, lax.shift_right_logical(values, jnp.int32(16)))
    return values


def gaussian_table(row_ids, col_ids, seed_value):
    row_hash = scramble(row_ids * 668265261 + seed_value)
    cell_hash = scramble(jnp.bitwise_xor(row_hash[:, None], col_ids[None, :] * 374761393))
    running = jnp.zeros(cell_hash.shape, jnp.float32)
    for stream in range(4):
        hashed = scramble(cell_hash + stream * 625341585)
        running = running + jnp.bitwise_and(hashed, 16777215).astype(jnp.float32) * (
            1.0 / 16777216.0
        )
    return (running - 2.0) * math.sqrt(3.0)


def gram_dot(left_side, right_side):
    return lax.dot_general(
        left_side, right_side, (((0,), (0,)), ((), ())), precision=PRECISE,
        preferred_element_type=jnp.float32,
    )


def dot(left_side, right_side):
    return jnp.dot(
        left_side, right_side, precision=PRECISE, preferred_element_type=jnp.float32
    )


def eliminate(blocks):
    size = blocks[0].shape[0]
    row_id = lax.broadcasted_iota(jnp.int32, (size, size), 0)
    col_id = lax.broadcasted_iota(jnp.int32, (size, size), 1)
    eye = jnp.where(row_id == col_id, 1.0, 0.0).astype(jnp.float32)
    work = [(block, eye) for block in blocks]
    for step in range(size - 1):
        later = []
        for block, inverse in work:
            pivot_row = block[step : step + 1, :]
            scaled = pivot_row / block[step : step + 1, step : step + 1]
            inv_row = inverse[step : step + 1, :] / block[step : step + 1, step : step + 1]
            column = jnp.where(row_id > step, block[:, step : step + 1], 0.0)
            later.append((block - column * scaled, inverse - column * inv_row))
        work = later
    factors = []
    for block, inverse in work:
        diagonal = jnp.sum(jnp.where(row_id == col_id, block, 0.0), axis=1, keepdims=True)
        factors.append(inverse / jnp.sqrt(diagonal))
    return factors


def factor_kernel(gram_ref, normal_ref, rhs_ref, factor_ref, out_ref, g, s, inv):
    n = gram_ref.shape[0]
    width = rhs_ref.shape[1]
    g[...] = gram_ref[...]
    s[:, :n] = normal_ref[...]
    s[:, n:] = rhs_ref[...]
    factor_ref[...] = jnp.zeros_like(factor_ref)
    for lo in range(0, n, BLOCK):
        hi = lo + BLOCK
        base = lo // 128 * 128
        first, second = eliminate([g[lo:hi, lo:hi], s[lo:hi, lo:hi]])
        inv[lo:hi, :] = second
        g_panel = dot(first, g[lo:hi, base:])
        s_panel = dot(second, s[lo:hi, base:])
        s[lo:hi, base:] = s_panel
        rows = lax.broadcasted_iota(jnp.int32, g_panel.shape, 0) + lo
        cols = lax.broadcasted_iota(jnp.int32, g_panel.shape, 1) + base
        factor_ref[lo:hi, base:] = jnp.where(cols >= rows, g_panel, 0.0)
        if hi < n:
            after = hi // 128 * 128
            g[hi:, after:] -= gram_dot(g_panel[:, hi - base :], g_panel[:, after - base :])
            s[hi:, after:] -= gram_dot(s_panel[:, hi - base : n - base], s_panel[:, after - base :])
    for lo in range(n - BLOCK, -1, -BLOCK):
        hi = lo + BLOCK
        part = s[lo:hi, n:]
        if hi < n:
            part = part - dot(s[lo:hi, hi:n], out_ref[hi:, :])
        out_ref[lo:hi, :] = gram_dot(inv[lo:hi, :], part)


def factor_and_solve(gram, normal, rhs):
    n, width = rhs.shape
    return pl.pallas_call(
        factor_kernel,
        out_shape=(
            jax.ShapeDtypeStruct((n, n), jnp.float32),
            jax.ShapeDtypeStruct((n, width), jnp.float32),
        ),
        in_specs=[pl.BlockSpec(memory_space=pltpu.VMEM)] * 3,
        out_specs=(pl.BlockSpec(memory_space=pltpu.VMEM),) * 2,
        scratch_shapes=[
            pltpu.VMEM((n, n), jnp.float32),
            pltpu.VMEM((n, n + width), jnp.float32),
            pltpu.VMEM((n, BLOCK), jnp.float32),
        ],
        compiler_params=pltpu.CompilerParams(vmem_limit_bytes=40 * 1024 * 1024),
        name="factor_and_solve",
    )(gram, normal, rhs)


def local(snapshots, test_seeds, block_offsets):
    space_index = lax.axis_index("space")
    time_index = lax.axis_index("tm")
    cell_rows = snapshots.shape[0]
    snap_cols = snapshots.shape[1]
    cells_total = cell_rows * lax.axis_size("space")
    snaps_total = snap_cols * lax.axis_size("tm")
    cell_ids = (
        block_offsets[0] * cells_total
        + space_index * cell_rows
        + jnp.arange(cell_rows, dtype=jnp.int32)
    )
    snap_ids = (
        block_offsets[1] * snaps_total
        + time_index * snap_cols
        + jnp.arange(snap_cols, dtype=jnp.int32)
    )
    omega_test = gaussian_table(
        snap_ids, jnp.arange(RANGE, dtype=jnp.int32), test_seeds[0]
    ) / math.sqrt(cells_total * snaps_total)
    psi_test = gaussian_table(
        cell_ids, jnp.arange(CORANGE, dtype=jnp.int32), test_seeds[1]
    ) / math.sqrt(cells_total)
    psi_test = lax.optimization_barrier(psi_test)
    partial_range = jnp.dot(snapshots, omega_test, precision=PRECISE)
    range_sketch = lax.psum(partial_range, "tm")
    corange_sketch = lax.psum(gram_dot(psi_test, snapshots), "space")
    range_sketch, corange_sketch = lax.optimization_barrier((range_sketch, corange_sketch))
    mixed = lax.psum(gram_dot(psi_test, range_sketch), "space")
    gram = lax.psum(gram_dot(range_sketch, range_sketch), "space")
    normal = gram_dot(mixed, mixed)
    rhs = gram_dot(mixed, corange_sketch)
    factor, weights = factor_and_solve(gram, normal, rhs)
    residual = snapshots - jnp.dot(range_sketch, weights, precision=PRECISE)
    return (residual, factor)


def solution(mesh):
    return jax.shard_map(
        local,
        mesh=mesh,
        in_specs=(P("space", "tm"), P(), P()),
        out_specs=(P("space", "tm"), P()),
        check_vma=False,
    )
```

```python
import math

import jax
import jax.numpy as jnp
from jax import lax
from jax.experimental import pallas as pl
from jax.experimental.pallas import tpu as pltpu
from jax.sharding import PartitionSpec as P

RANGE = 512
CORANGE = 1024
BLOCK = 32

PRECISE = lax.Precision.HIGHEST


def scramble(values):
    values = jnp.bitwise_xor(values, lax.shift_right_logical(values, jnp.int32(16)))
    values = values * 73244475
    values = jnp.bitwise_xor(values, lax.shift_right_logical(values, jnp.int32(16)))
    values = values * 73244475
    values = jnp.bitwise_xor(values, lax.shift_right_logical(values, jnp.int32(16)))
    return values


def gaussian_table(row_ids, col_ids, seed_value):
    row_hash = scramble(row_ids * 668265261 + seed_value)
    cell_hash = scramble(jnp.bitwise_xor(row_hash[:, None], col_ids[None, :] * 374761393))
    running = jnp.zeros(cell_hash.shape, jnp.float32)
    for stream in range(4):
        hashed = scramble(cell_hash + stream * 625341585)
        running = running + jnp.bitwise_and(hashed, 16777215).astype(jnp.float32) * (
            1.0 / 16777216.0
        )
    return (running - 2.0) * math.sqrt(3.0)


def gram_dot(left_side, right_side):
    return lax.dot_general(
        left_side, right_side, (((0,), (0,)), ((), ())), precision=PRECISE,
        preferred_element_type=jnp.float32,
    )


def dot(left_side, right_side):
    return jnp.dot(
        left_side, right_side, precision=PRECISE, preferred_element_type=jnp.float32
    )


def eliminate(blocks):
    size = blocks[0].shape[0]
    row_id = lax.broadcasted_iota(jnp.int32, (size, size), 0)
    col_id = lax.broadcasted_iota(jnp.int32, (size, size), 1)
    eye = jnp.where(row_id == col_id, 1.0, 0.0).astype(jnp.float32)
    work = [(block, eye) for block in blocks]
    for step in range(size - 1):
        later = []
        for block, inverse in work:
            pivot_row = block[step : step + 1, :]
            scaled = pivot_row / block[step : step + 1, step : step + 1]
            inv_row = inverse[step : step + 1, :] / block[step : step + 1, step : step + 1]
            column = jnp.where(row_id > step, block[:, step : step + 1], 0.0)
            later.append((block - column * scaled, inverse - column * inv_row))
        work = later
    factors = []
    for block, inverse in work:
        diagonal = jnp.sum(jnp.where(row_id == col_id, block, 0.0), axis=1, keepdims=True)
        factors.append(inverse / jnp.sqrt(diagonal))
    return factors


def factor_kernel(gram_ref, normal_ref, rhs_ref, factor_ref, out_ref, g, s, inv):
    n = gram_ref.shape[0]
    width = rhs_ref.shape[1]
    g[...] = gram_ref[...]
    s[:, :n] = normal_ref[...]
    s[:, n:] = rhs_ref[...]
    factor_ref[...] = jnp.zeros_like(factor_ref)
    for lo in range(0, n, BLOCK):
        hi = lo + BLOCK
        base = lo // 128 * 128
        first, second = eliminate([g[lo:hi, lo:hi], s[lo:hi, lo:hi]])
        inv[lo:hi, :] = second
        g_panel = dot(first, g[lo:hi, base:])
        s_panel = dot(second, s[lo:hi, base:])
        s[lo:hi, base:] = s_panel
        rows = lax.broadcasted_iota(jnp.int32, g_panel.shape, 0) + lo
        cols = lax.broadcasted_iota(jnp.int32, g_panel.shape, 1) + base
        factor_ref[lo:hi, base:] = jnp.where(cols >= rows, g_panel, 0.0)
        if hi < n:
            after = hi // 128 * 128
            g[hi:, after:] -= gram_dot(g_panel[:, hi - base :], g_panel[:, after - base :])
            s[hi:, after:] -= gram_dot(s_panel[:, hi - base : n - base], s_panel[:, after - base :])
    for lo in range(n - BLOCK, -1, -BLOCK):
        hi = lo + BLOCK
        part = s[lo:hi, n:]
        if hi < n:
            part = part - dot(s[lo:hi, hi:n], out_ref[hi:, :])
        out_ref[lo:hi, :] = gram_dot(inv[lo:hi, :], part)


def factor_and_solve(gram, normal, rhs):
    n, width = rhs.shape
    return pl.pallas_call(
        factor_kernel,
        out_shape=(
            jax.ShapeDtypeStruct((n, n), jnp.float32),
            jax.ShapeDtypeStruct((n, width), jnp.float32),
        ),
        in_specs=[pl.BlockSpec(memory_space=pltpu.VMEM)] * 3,
        out_specs=(pl.BlockSpec(memory_space=pltpu.VMEM),) * 2,
        scratch_shapes=[
            pltpu.VMEM((n, n), jnp.float32),
            pltpu.VMEM((n, n + width), jnp.float32),
            pltpu.VMEM((n, BLOCK), jnp.float32),
        ],
        compiler_params=pltpu.CompilerParams(vmem_limit_bytes=40 * 1024 * 1024),
        cost_estimate=pl.CostEstimate(
            flops=20 * n * n * (n + width), bytes_accessed=20 * n * n, transcendentals=0
        ),
        name="factor_and_solve",
    )(gram, normal, rhs)


def local(snapshots, test_seeds, block_offsets):
    space_index = lax.axis_index("space")
    time_index = lax.axis_index("tm")
    cell_rows = snapshots.shape[0]
    snap_cols = snapshots.shape[1]
    cells_total = cell_rows * lax.axis_size("space")
    snaps_total = snap_cols * lax.axis_size("tm")
    cell_ids = (
        block_offsets[0] * cells_total
        + space_index * cell_rows
        + jnp.arange(cell_rows, dtype=jnp.int32)
    )
    snap_ids = (
        block_offsets[1] * snaps_total
        + time_index * snap_cols
        + jnp.arange(snap_cols, dtype=jnp.int32)
    )
    omega_test = gaussian_table(
        snap_ids, jnp.arange(RANGE, dtype=jnp.int32), test_seeds[0]
    ) / math.sqrt(cells_total * snaps_total)
    psi_test = gaussian_table(
        cell_ids, jnp.arange(CORANGE, dtype=jnp.int32), test_seeds[1]
    ) / math.sqrt(cells_total)
    psi_test = lax.optimization_barrier(psi_test)
    partial_range = jnp.dot(snapshots, omega_test, precision=PRECISE)
    range_sketch = lax.psum(partial_range, "tm")
    corange_part = gram_dot(psi_test, snapshots)
    range_sketch, corange_part = lax.optimization_barrier((range_sketch, corange_part))
    half = RANGE // 2
    side = lax.rem(time_index, 2)
    mine = lax.dynamic_slice_in_dim(range_sketch, side * half, half, axis=1)
    product = lax.psum(
        jnp.concatenate([gram_dot(psi_test, mine), gram_dot(range_sketch, mine)], axis=0),
        "space",
    )
    pairs = [(index, index ^ 1) for index in range(lax.axis_size("tm"))]
    other = lax.ppermute(product, "tm", pairs)
    left = jnp.where(side == 0, product, other)
    right = jnp.where(side == 0, other, product)
    mixed = jnp.concatenate([left[:CORANGE], right[:CORANGE]], axis=1)
    gram = jnp.concatenate([left[CORANGE:], right[CORANGE:]], axis=1)
    rhs = lax.psum(gram_dot(mixed, corange_part), "space")
    normal = gram_dot(mixed, mixed)
    factor, inverse = factor_and_solve(gram, normal, jnp.eye(RANGE, dtype=jnp.float32))
    weights = jnp.dot(inverse, rhs, precision=PRECISE)
    residual = snapshots - jnp.dot(range_sketch, weights, precision=PRECISE)
    return (residual, factor)


def solution(mesh):
    return jax.shard_map(
        local,
        mesh=mesh,
        in_specs=(P("space", "tm"), P(), P()),
        out_specs=(P("space", "tm"), P()),
        check_vma=False,
    )
```

```python
import math

import jax
import jax.numpy as jnp
from jax import lax
from jax.experimental import pallas as pl
from jax.experimental.pallas import tpu as pltpu
from jax.sharding import PartitionSpec as P

RANGE = 512
CORANGE = 1024
BLOCK = 32

PRECISE = lax.Precision.HIGHEST


def scramble(values):
    values = jnp.bitwise_xor(values, lax.shift_right_logical(values, jnp.int32(16)))
    values = values * 73244475
    values = jnp.bitwise_xor(values, lax.shift_right_logical(values, jnp.int32(16)))
    values = values * 73244475
    values = jnp.bitwise_xor(values, lax.shift_right_logical(values, jnp.int32(16)))
    return values


def gaussian_table(row_ids, col_ids, seed_value):
    row_hash = scramble(row_ids * 668265261 + seed_value)
    cell_hash = scramble(jnp.bitwise_xor(row_hash[:, None], col_ids[None, :] * 374761393))
    running = jnp.zeros(cell_hash.shape, jnp.float32)
    for stream in range(4):
        hashed = scramble(cell_hash + stream * 625341585)
        running = running + jnp.bitwise_and(hashed, 16777215).astype(jnp.float32) * (
            1.0 / 16777216.0
        )
    return (running - 2.0) * math.sqrt(3.0)


def gram_dot(left_side, right_side):
    return lax.dot_general(
        left_side, right_side, (((0,), (0,)), ((), ())), precision=PRECISE,
        preferred_element_type=jnp.float32,
    )


def dot(left_side, right_side):
    return jnp.dot(
        left_side, right_side, precision=PRECISE, preferred_element_type=jnp.float32
    )


def eliminate(blocks):
    size = blocks[0].shape[0]
    row_id = lax.broadcasted_iota(jnp.int32, (size, size), 0)
    col_id = lax.broadcasted_iota(jnp.int32, (size, size), 1)
    eye = jnp.where(row_id == col_id, 1.0, 0.0).astype(jnp.float32)
    work = [(block, eye) for block in blocks]
    for step in range(size - 1):
        later = []
        for block, inverse in work:
            pivot_row = block[step : step + 1, :]
            scaled = pivot_row / block[step : step + 1, step : step + 1]
            inv_row = inverse[step : step + 1, :] / block[step : step + 1, step : step + 1]
            column = jnp.where(row_id > step, block[:, step : step + 1], 0.0)
            later.append((block - column * scaled, inverse - column * inv_row))
        work = later
    factors = []
    for block, inverse in work:
        diagonal = jnp.sum(jnp.where(row_id == col_id, block, 0.0), axis=1, keepdims=True)
        factors.append(inverse / jnp.sqrt(diagonal))
    return factors


def factor_kernel(gram_ref, normal_ref, factor_ref, out_ref, g, s):
    n = gram_ref.shape[0]
    tile = 128

    def identity(shape):
        rows = lax.broadcasted_iota(jnp.int32, shape, 0)
        cols = lax.broadcasted_iota(jnp.int32, shape, 1)
        return jnp.where(rows == cols, 1.0, 0.0).astype(jnp.float32)

    g[...] = gram_ref[...]
    s[:, :n] = normal_ref[...]
    s[:, n:] = identity((n, n))

    @pl.loop(0, n // tile)
    def _(index):
        base = pl.multiple_of(index * tile, tile)
        here = pl.ds(base, tile)
        works = [
            jnp.concatenate([ref[here, here], identity((tile, tile))], axis=1) for ref in (g, s)
        ]
        done = [[], []]
        for lo in range(0, tile, BLOCK):
            smalls = eliminate([work[:BLOCK, lo : lo + BLOCK] for work in works])
            for place in range(2):
                rows = dot(smalls[place], works[place][:BLOCK])
                done[place].append(rows[:, tile:])
                if lo + BLOCK < tile:
                    works[place] = works[place][BLOCK:] - gram_dot(
                        rows[:, lo + BLOCK : tile], rows
                    )
        g_panel = dot(jnp.concatenate(done[0], axis=0), g[here, :])
        s_panel = dot(jnp.concatenate(done[1], axis=0), s[here, :])
        rows = lax.broadcasted_iota(jnp.int32, g_panel.shape, 0) + base
        cols = lax.broadcasted_iota(jnp.int32, g_panel.shape, 1)
        factor_ref[here, :] = jnp.where(cols >= rows, g_panel, 0.0)
        after = cols >= base + tile
        g[...] -= gram_dot(jnp.where(after, g_panel, 0.0), g_panel)
        s[...] -= gram_dot(jnp.where(after, s_panel[:, :n], 0.0), s_panel)
        s[here, :] = s_panel

    out_ref[...] = gram_dot(s[:, n:], s[:, n:])


def factor_and_invert(gram, normal):
    n = gram.shape[0]
    return pl.pallas_call(
        factor_kernel,
        out_shape=(jax.ShapeDtypeStruct((n, n), jnp.float32),) * 2,
        in_specs=[pl.BlockSpec(memory_space=pltpu.VMEM)] * 2,
        out_specs=(pl.BlockSpec(memory_space=pltpu.VMEM),) * 2,
        scratch_shapes=[
            pltpu.VMEM((n, n), jnp.float32),
            pltpu.VMEM((n, 2 * n), jnp.float32),
        ],
        compiler_params=pltpu.CompilerParams(vmem_limit_bytes=40 * 1024 * 1024),
        cost_estimate=pl.CostEstimate(
            flops=40 * n * n * n, bytes_accessed=20 * n * n, transcendentals=0
        ),
        name="factor_and_invert",
    )(gram, normal)


def butterfly_sum(parts, axis):
    size = lax.axis_size(axis)
    levels = size.bit_length() - 1
    position = lax.axis_index(axis)
    orders = [list(range(levels)), list(range(levels))[::-1]]
    parts = list(parts)

    def swap(value, level):
        return lax.ppermute(value, axis, [(i, i ^ (1 << level)) for i in range(size)])

    def side(level):
        return jnp.bitwise_and(lax.shift_right_logical(position, level), 1)

    for turn in range(levels):
        for place, order in enumerate(orders):
            level = order[turn]
            value = parts[place]
            rows = value.shape[0] // 2
            keep = lax.dynamic_slice_in_dim(value, side(level) * rows, rows, axis=0)
            give = lax.dynamic_slice_in_dim(value, (1 - side(level)) * rows, rows, axis=0)
            parts[place] = keep + swap(give, level)
    for turn in reversed(range(levels)):
        for place, order in enumerate(orders):
            level = order[turn]
            value = parts[place]
            other = swap(value, level)
            first = side(level) == 0
            parts[place] = jnp.concatenate(
                [jnp.where(first, value, other), jnp.where(first, other, value)], axis=0
            )
    return parts


def local(snapshots, test_seeds, block_offsets):
    space_index = lax.axis_index("space")
    time_index = lax.axis_index("tm")
    cell_rows = snapshots.shape[0]
    snap_cols = snapshots.shape[1]
    cells_total = cell_rows * lax.axis_size("space")
    snaps_total = snap_cols * lax.axis_size("tm")
    cell_ids = (
        block_offsets[0] * cells_total
        + space_index * cell_rows
        + jnp.arange(cell_rows, dtype=jnp.int32)
    )
    snap_ids = (
        block_offsets[1] * snaps_total
        + time_index * snap_cols
        + jnp.arange(snap_cols, dtype=jnp.int32)
    )
    omega_test = gaussian_table(
        snap_ids, jnp.arange(RANGE, dtype=jnp.int32), test_seeds[0]
    ) / math.sqrt(cells_total * snaps_total)
    psi_test = gaussian_table(
        cell_ids, jnp.arange(CORANGE, dtype=jnp.int32), test_seeds[1]
    ) / math.sqrt(cells_total)
    psi_test = lax.optimization_barrier(psi_test)
    partial_range = jnp.dot(snapshots, omega_test, precision=PRECISE)
    range_sketch = lax.psum(partial_range, "tm")
    corange_part = gram_dot(psi_test, snapshots)
    range_sketch, corange_part = lax.optimization_barrier((range_sketch, corange_part))
    half = RANGE // 2
    side = lax.rem(time_index, 2)
    mine = lax.dynamic_slice_in_dim(range_sketch, side * half, half, axis=1)
    cut = (CORANGE + RANGE) // 2
    stacked = jnp.concatenate(
        [gram_dot(psi_test, mine), gram_dot(range_sketch, mine)], axis=0
    )
    product = jnp.concatenate(butterfly_sum([stacked[:cut], stacked[cut:]], "space"), axis=0)
    pairs = [(index, index ^ 1) for index in range(lax.axis_size("tm"))]
    other = lax.ppermute(product, "tm", pairs)
    left = jnp.where(side == 0, product, other)
    right = jnp.where(side == 0, other, product)
    mixed = jnp.concatenate([left[:CORANGE], right[:CORANGE]], axis=1)
    gram = jnp.concatenate([left[CORANGE:], right[CORANGE:]], axis=1)
    rhs = lax.psum(gram_dot(mixed, corange_part), "space")
    normal = gram_dot(mixed, mixed)
    factor, inverse = factor_and_invert(gram, normal)
    weights = jnp.dot(inverse, rhs, precision=PRECISE)
    residual = snapshots - jnp.dot(range_sketch, weights, precision=PRECISE)
    return (residual, factor)


def solution(mesh):
    return jax.shard_map(
        local,
        mesh=mesh,
        in_specs=(P("space", "tm"), P(), P()),
        out_specs=(P("space", "tm"), P()),
        check_vma=False,
    )
```

```python
import math

import jax
import jax.numpy as jnp
from jax import lax
from jax.experimental import pallas as pl
from jax.experimental.pallas import tpu as pltpu
from jax.sharding import PartitionSpec as P

RANGE = 512
CORANGE = 1024
BLOCK = 32
GROUP = 8

PRECISE = lax.Precision.HIGHEST


def scramble(values):
    values = jnp.bitwise_xor(values, lax.shift_right_logical(values, jnp.int32(16)))
    values = values * 73244475
    values = jnp.bitwise_xor(values, lax.shift_right_logical(values, jnp.int32(16)))
    values = values * 73244475
    values = jnp.bitwise_xor(values, lax.shift_right_logical(values, jnp.int32(16)))
    return values


def gaussian_table(row_ids, col_ids, seed_value):
    row_hash = scramble(row_ids * 668265261 + seed_value)
    cell_hash = scramble(jnp.bitwise_xor(row_hash[:, None], col_ids[None, :] * 374761393))
    running = jnp.zeros(cell_hash.shape, jnp.float32)
    for stream in range(4):
        hashed = scramble(cell_hash + stream * 625341585)
        running = running + jnp.bitwise_and(hashed, 16777215).astype(jnp.float32) * (
            1.0 / 16777216.0
        )
    return (running - 2.0) * math.sqrt(3.0)


def gram_dot(left_side, right_side):
    return lax.dot_general(
        left_side, right_side, (((0,), (0,)), ((), ())), precision=PRECISE,
        preferred_element_type=jnp.float32,
    )


def dot(left_side, right_side):
    return jnp.dot(
        left_side, right_side, precision=PRECISE, preferred_element_type=jnp.float32
    )


def eliminate(blocks):
    size = blocks[0].shape[0]
    row_id = lax.broadcasted_iota(jnp.int32, (size, size), 0)
    col_id = lax.broadcasted_iota(jnp.int32, (size, size), 1)
    eye = jnp.where(row_id == col_id, 1.0, 0.0).astype(jnp.float32)
    work = [(block, eye) for block in blocks]
    for start in range(0, size, GROUP):
        columns = [
            [
                jnp.broadcast_to(block[:, start + j : start + j + 1], (size, size))
                for j in range(GROUP)
            ]
            for block, _ in work
        ]
        for j in range(GROUP):
            step = start + j
            later = []
            for (block, inverse), column in zip(work, columns):
                below = jnp.where(row_id > step, column[j], 0.0)
                share = below * (1.0 / column[j][step : step + 1, :])
                for i in range(j + 1, GROUP):
                    column[i] = column[i] - share * column[i][step : step + 1, :]
                later.append(
                    (
                        block - share * block[step : step + 1, :],
                        inverse - share * inverse[step : step + 1, :],
                    )
                )
            work = later
    factors = []
    for block, inverse in work:
        diagonal = jnp.sum(jnp.where(row_id == col_id, block, 0.0), axis=1, keepdims=True)
        factors.append(inverse / jnp.sqrt(diagonal))
    return factors


def factor_kernel(gram_ref, normal_ref, factor_ref, out_ref, g, s):
    n = gram_ref.shape[0]
    tile = 128

    def identity(shape):
        rows = lax.broadcasted_iota(jnp.int32, shape, 0)
        cols = lax.broadcasted_iota(jnp.int32, shape, 1)
        return jnp.where(rows == cols, 1.0, 0.0).astype(jnp.float32)

    g[...] = gram_ref[...]
    s[:, :n] = normal_ref[...]
    s[:, n:] = identity((n, n))

    @pl.loop(0, n // tile)
    def _(index):
        base = pl.multiple_of(index * tile, tile)
        here = pl.ds(base, tile)
        works = [
            jnp.concatenate([ref[here, here], identity((tile, tile))], axis=1) for ref in (g, s)
        ]
        done = [[], []]
        for lo in range(0, tile, BLOCK):
            smalls = eliminate([work[:BLOCK, lo : lo + BLOCK] for work in works])
            for place in range(2):
                rows = dot(smalls[place], works[place][:BLOCK])
                done[place].append(rows[:, tile:])
                if lo + BLOCK < tile:
                    works[place] = works[place][BLOCK:] - gram_dot(
                        rows[:, lo + BLOCK : tile], rows
                    )
        g_panel = dot(jnp.concatenate(done[0], axis=0), g[here, :])
        s_panel = dot(jnp.concatenate(done[1], axis=0), s[here, :])
        rows = lax.broadcasted_iota(jnp.int32, g_panel.shape, 0) + base
        cols = lax.broadcasted_iota(jnp.int32, g_panel.shape, 1)
        factor_ref[here, :] = jnp.where(cols >= rows, g_panel, 0.0)
        after = cols >= base + tile
        g[...] -= gram_dot(jnp.where(after, g_panel, 0.0), g_panel)
        s[...] -= gram_dot(jnp.where(after, s_panel[:, :n], 0.0), s_panel)
        s[here, :] = s_panel

    out_ref[...] = gram_dot(s[:, n:], s[:, n:])


def factor_and_invert(gram, normal):
    n = gram.shape[0]
    return pl.pallas_call(
        factor_kernel,
        out_shape=(jax.ShapeDtypeStruct((n, n), jnp.float32),) * 2,
        in_specs=[pl.BlockSpec(memory_space=pltpu.VMEM)] * 2,
        out_specs=(pl.BlockSpec(memory_space=pltpu.VMEM),) * 2,
        scratch_shapes=[
            pltpu.VMEM((n, n), jnp.float32),
            pltpu.VMEM((n, 2 * n), jnp.float32),
        ],
        compiler_params=pltpu.CompilerParams(vmem_limit_bytes=40 * 1024 * 1024),
        cost_estimate=pl.CostEstimate(
            flops=40 * n * n * n, bytes_accessed=20 * n * n, transcendentals=0
        ),
        name="factor_and_invert",
    )(gram, normal)


def butterfly_sum(parts, axis, lowest=0):
    size = lax.axis_size(axis)
    bits = list(range(lowest, size.bit_length() - 1))
    levels = len(bits)
    position = lax.axis_index(axis)
    orders = [bits, bits[::-1]]
    parts = list(parts)

    def swap(value, level):
        return lax.ppermute(value, axis, [(i, i ^ (1 << level)) for i in range(size)])

    def side(level):
        return jnp.bitwise_and(lax.shift_right_logical(position, level), 1)

    for turn in range(levels):
        for place, order in enumerate(orders):
            level = order[turn]
            value = parts[place]
            rows = value.shape[0] // 2
            keep = lax.dynamic_slice_in_dim(value, side(level) * rows, rows, axis=0)
            give = lax.dynamic_slice_in_dim(value, (1 - side(level)) * rows, rows, axis=0)
            parts[place] = keep + swap(give, level)
    for turn in reversed(range(levels)):
        for place, order in enumerate(orders):
            level = order[turn]
            value = parts[place]
            other = swap(value, level)
            first = side(level) == 0
            parts[place] = jnp.concatenate(
                [jnp.where(first, value, other), jnp.where(first, other, value)], axis=0
            )
    return parts


def local(snapshots, test_seeds, block_offsets):
    space_index = lax.axis_index("space")
    time_index = lax.axis_index("tm")
    cell_rows = snapshots.shape[0]
    snap_cols = snapshots.shape[1]
    cells_total = cell_rows * lax.axis_size("space")
    snaps_total = snap_cols * lax.axis_size("tm")
    cell_ids = (
        block_offsets[0] * cells_total
        + space_index * cell_rows
        + jnp.arange(cell_rows, dtype=jnp.int32)
    )
    snap_ids = (
        block_offsets[1] * snaps_total
        + time_index * snap_cols
        + jnp.arange(snap_cols, dtype=jnp.int32)
    )
    omega_test = gaussian_table(
        snap_ids, jnp.arange(RANGE, dtype=jnp.int32), test_seeds[0]
    ) / math.sqrt(cells_total * snaps_total)
    psi_test = gaussian_table(
        cell_ids, jnp.arange(CORANGE, dtype=jnp.int32), test_seeds[1]
    ) / math.sqrt(cells_total)
    psi_test = lax.optimization_barrier(psi_test)
    partial_range = jnp.dot(snapshots, omega_test, precision=PRECISE)
    half = RANGE // 2
    side = lax.rem(time_index, 2)
    pairs = [(index, index ^ 1) for index in range(lax.axis_size("tm"))]
    keep = lax.dynamic_slice_in_dim(partial_range, side * half, half, axis=1)
    give = lax.dynamic_slice_in_dim(partial_range, (1 - side) * half, half, axis=1)
    mine = keep + lax.ppermute(give, "tm", pairs)
    middle = cell_rows // 2
    mine = jnp.concatenate(butterfly_sum([mine[:middle], mine[middle:]], "tm", 1), axis=0)
    corange_part = gram_dot(psi_test, snapshots)
    mine, corange_part = lax.optimization_barrier((mine, corange_part))
    swapped = lax.ppermute(mine, "tm", pairs)
    range_sketch = jnp.concatenate(
        [jnp.where(side == 0, mine, swapped), jnp.where(side == 0, swapped, mine)], axis=1
    )
    cut = (CORANGE + RANGE) // 2
    stacked = jnp.concatenate(
        [gram_dot(psi_test, mine), gram_dot(range_sketch, mine)], axis=0
    )
    product = jnp.concatenate(butterfly_sum([stacked[:cut], stacked[cut:]], "space"), axis=0)
    other = lax.ppermute(product, "tm", pairs)
    left = jnp.where(side == 0, product, other)
    right = jnp.where(side == 0, other, product)
    mixed = jnp.concatenate([left[:CORANGE], right[:CORANGE]], axis=1)
    gram = jnp.concatenate([left[CORANGE:], right[CORANGE:]], axis=1)
    rhs = lax.psum(gram_dot(mixed, corange_part), "space")
    normal = gram_dot(mixed, mixed)
    factor, inverse = factor_and_invert(gram, normal)
    weights = jnp.dot(inverse, rhs, precision=PRECISE)
    residual = snapshots - jnp.dot(range_sketch, weights, precision=PRECISE)
    return (residual, factor)


def solution(mesh):
    return jax.shard_map(
        local,
        mesh=mesh,
        in_specs=(P("space", "tm"), P(), P()),
        out_specs=(P("space", "tm"), P()),
        check_vma=False,
    )
```

```python
import math

import jax
import jax.numpy as jnp
from jax import lax
from jax.experimental import pallas as pl
from jax.experimental.pallas import tpu as pltpu
from jax.sharding import PartitionSpec as P

RANGE = 512
CORANGE = 1024
BLOCK = 32
GROUP = 8

PRECISE = lax.Precision.HIGHEST
SPLIT = lax.Precision.HIGH


def scramble(values):
    values = jnp.bitwise_xor(values, lax.shift_right_logical(values, jnp.int32(16)))
    values = values * 73244475
    values = jnp.bitwise_xor(values, lax.shift_right_logical(values, jnp.int32(16)))
    values = values * 73244475
    values = jnp.bitwise_xor(values, lax.shift_right_logical(values, jnp.int32(16)))
    return values


def gaussian_table(row_ids, col_ids, seed_value):
    row_hash = scramble(row_ids * 668265261 + seed_value)
    cell_hash = scramble(jnp.bitwise_xor(row_hash[:, None], col_ids[None, :] * 374761393))
    running = jnp.zeros(cell_hash.shape, jnp.float32)
    for stream in range(4):
        hashed = scramble(cell_hash + stream * 625341585)
        running = running + jnp.bitwise_and(hashed, 16777215).astype(jnp.float32) * (
            1.0 / 16777216.0
        )
    return (running - 2.0) * math.sqrt(3.0)


def gram_dot(left_side, right_side):
    return lax.dot_general(
        left_side, right_side, (((0,), (0,)), ((), ())), precision=PRECISE,
        preferred_element_type=jnp.float32,
    )


def dot(left_side, right_side):
    return jnp.dot(
        left_side, right_side, precision=PRECISE, preferred_element_type=jnp.float32
    )


def eliminate(blocks):
    size = blocks[0].shape[0]
    row_id = lax.broadcasted_iota(jnp.int32, (size, size), 0)
    col_id = lax.broadcasted_iota(jnp.int32, (size, size), 1)
    eye = jnp.where(row_id == col_id, 1.0, 0.0).astype(jnp.float32)
    work = [(block, eye) for block in blocks]
    for start in range(0, size, GROUP):
        columns = [
            [
                jnp.broadcast_to(block[:, start + j : start + j + 1], (size, size))
                for j in range(GROUP)
            ]
            for block, _ in work
        ]
        for j in range(GROUP):
            step = start + j
            later = []
            for (block, inverse), column in zip(work, columns):
                below = jnp.where(row_id > step, column[j], 0.0)
                share = below * (1.0 / column[j][step : step + 1, :])
                for i in range(j + 1, GROUP):
                    column[i] = column[i] - share * column[i][step : step + 1, :]
                later.append(
                    (
                        block - share * block[step : step + 1, :],
                        inverse - share * inverse[step : step + 1, :],
                    )
                )
            work = later
    factors = []
    for block, inverse in work:
        diagonal = jnp.sum(jnp.where(row_id == col_id, block, 0.0), axis=1, keepdims=True)
        factors.append(inverse / jnp.sqrt(diagonal))
    return factors


def factor_kernel(gram_ref, normal_ref, factor_ref, out_ref, g, s):
    n = gram_ref.shape[0]
    tile = 128

    def identity(shape):
        rows = lax.broadcasted_iota(jnp.int32, shape, 0)
        cols = lax.broadcasted_iota(jnp.int32, shape, 1)
        return jnp.where(rows == cols, 1.0, 0.0).astype(jnp.float32)

    g[...] = gram_ref[...]
    s[:, :n] = normal_ref[...]
    s[:, n:] = identity((n, n))

    @pl.loop(0, n // tile)
    def _(index):
        base = pl.multiple_of(index * tile, tile)
        here = pl.ds(base, tile)
        works = [
            jnp.concatenate([ref[here, here], identity((tile, tile))], axis=1) for ref in (g, s)
        ]
        done = [[], []]
        for lo in range(0, tile, BLOCK):
            smalls = eliminate([work[:BLOCK, lo : lo + BLOCK] for work in works])
            for place in range(2):
                rows = dot(smalls[place], works[place][:BLOCK])
                done[place].append(rows[:, tile:])
                if lo + BLOCK < tile:
                    works[place] = works[place][BLOCK:] - gram_dot(
                        rows[:, lo + BLOCK : tile], rows
                    )
        g_panel = dot(jnp.concatenate(done[0], axis=0), g[here, :])
        s_panel = dot(jnp.concatenate(done[1], axis=0), s[here, :])
        rows = lax.broadcasted_iota(jnp.int32, g_panel.shape, 0) + base
        cols = lax.broadcasted_iota(jnp.int32, g_panel.shape, 1)
        factor_ref[here, :] = jnp.where(cols >= rows, g_panel, 0.0)
        after = cols >= base + tile
        g[...] -= gram_dot(jnp.where(after, g_panel, 0.0), g_panel)
        s[...] -= gram_dot(jnp.where(after, s_panel[:, :n], 0.0), s_panel)
        s[here, :] = s_panel

    out_ref[...] = gram_dot(s[:, n:], s[:, n:])


def factor_and_invert(gram, normal):
    n = gram.shape[0]
    return pl.pallas_call(
        factor_kernel,
        out_shape=(jax.ShapeDtypeStruct((n, n), jnp.float32),) * 2,
        in_specs=[pl.BlockSpec(memory_space=pltpu.VMEM)] * 2,
        out_specs=(pl.BlockSpec(memory_space=pltpu.VMEM),) * 2,
        scratch_shapes=[
            pltpu.VMEM((n, n), jnp.float32),
            pltpu.VMEM((n, 2 * n), jnp.float32),
        ],
        compiler_params=pltpu.CompilerParams(vmem_limit_bytes=40 * 1024 * 1024),
        cost_estimate=pl.CostEstimate(
            flops=40 * n * n * n, bytes_accessed=20 * n * n, transcendentals=0
        ),
        name="factor_and_invert",
    )(gram, normal)


def butterfly_sum(parts, axis, lowest=0):
    size = lax.axis_size(axis)
    bits = list(range(lowest, size.bit_length() - 1))
    levels = len(bits)
    position = lax.axis_index(axis)
    orders = [bits, bits[::-1]]
    parts = list(parts)

    def swap(value, level):
        return lax.ppermute(value, axis, [(i, i ^ (1 << level)) for i in range(size)])

    def side(level):
        return jnp.bitwise_and(lax.shift_right_logical(position, level), 1)

    for turn in range(levels):
        for place, order in enumerate(orders):
            level = order[turn]
            value = parts[place]
            rows = value.shape[0] // 2
            keep = lax.dynamic_slice_in_dim(value, side(level) * rows, rows, axis=0)
            give = lax.dynamic_slice_in_dim(value, (1 - side(level)) * rows, rows, axis=0)
            parts[place] = keep + swap(give, level)
    for turn in reversed(range(levels)):
        for place, order in enumerate(orders):
            level = order[turn]
            value = parts[place]
            other = swap(value, level)
            first = side(level) == 0
            parts[place] = jnp.concatenate(
                [jnp.where(first, value, other), jnp.where(first, other, value)], axis=0
            )
    return parts


def local(snapshots, test_seeds, block_offsets):
    space_index = lax.axis_index("space")
    time_index = lax.axis_index("tm")
    cell_rows = snapshots.shape[0]
    snap_cols = snapshots.shape[1]
    cells_total = cell_rows * lax.axis_size("space")
    snaps_total = snap_cols * lax.axis_size("tm")
    cell_ids = (
        block_offsets[0] * cells_total
        + space_index * cell_rows
        + jnp.arange(cell_rows, dtype=jnp.int32)
    )
    snap_ids = (
        block_offsets[1] * snaps_total
        + time_index * snap_cols
        + jnp.arange(snap_cols, dtype=jnp.int32)
    )
    omega_test = gaussian_table(
        snap_ids, jnp.arange(RANGE, dtype=jnp.int32), test_seeds[0]
    ) / math.sqrt(cells_total * snaps_total)
    psi_test = gaussian_table(
        cell_ids, jnp.arange(CORANGE, dtype=jnp.int32), test_seeds[1]
    ) / math.sqrt(cells_total)
    psi_test = lax.optimization_barrier(psi_test)
    partial_range = jnp.dot(snapshots, omega_test, precision=SPLIT)
    half = RANGE // 2
    side = lax.rem(time_index, 2)
    pairs = [(index, index ^ 1) for index in range(lax.axis_size("tm"))]
    keep = lax.dynamic_slice_in_dim(partial_range, side * half, half, axis=1)
    give = lax.dynamic_slice_in_dim(partial_range, (1 - side) * half, half, axis=1)
    mine = keep + lax.ppermute(give, "tm", pairs)
    middle = cell_rows // 2
    mine = jnp.concatenate(butterfly_sum([mine[:middle], mine[middle:]], "tm", 1), axis=0)
    corange_part = lax.dot_general(
        psi_test, snapshots, (((0,), (0,)), ((), ())), precision=SPLIT
    )
    mine, corange_part = lax.optimization_barrier((mine, corange_part))
    swapped = lax.ppermute(mine, "tm", pairs)
    range_sketch = jnp.concatenate(
        [jnp.where(side == 0, mine, swapped), jnp.where(side == 0, swapped, mine)], axis=1
    )
    cut = (CORANGE + RANGE) // 2
    stacked = jnp.concatenate(
        [gram_dot(psi_test, mine), gram_dot(range_sketch, mine)], axis=0
    )
    product = jnp.concatenate(butterfly_sum([stacked[:cut], stacked[cut:]], "space"), axis=0)
    other = lax.ppermute(product, "tm", pairs)
    left = jnp.where(side == 0, product, other)
    right = jnp.where(side == 0, other, product)
    mixed = jnp.concatenate([left[:CORANGE], right[:CORANGE]], axis=1)
    gram = jnp.concatenate([left[CORANGE:], right[CORANGE:]], axis=1)
    rhs = lax.psum(gram_dot(mixed, corange_part), "space")
    normal = gram_dot(mixed, mixed)
    factor, inverse = factor_and_invert(gram, normal)
    weights = jnp.dot(inverse, rhs, precision=PRECISE)
    residual = snapshots - jnp.dot(range_sketch, weights, precision=SPLIT)
    return (residual, factor)


def solution(mesh):
    return jax.shard_map(
        local,
        mesh=mesh,
        in_specs=(P("space", "tm"), P(), P()),
        out_specs=(P("space", "tm"), P()),
        check_vma=False,
    )
```
